128 devices in a mesh: front: 4 (over z), tile: 32 (over x, y, core).
Axes of the slice: x: 4, y: 4, z: 4, core: 2. Of those that a mesh axis runs over, the one named last changes fastest.
Arguments:
- front_entries: float32 [4, 4096, 4096], P('front', 'tile')
- child_blocks: bfloat16 [512, 64, 256], P(('front', 'tile'))
- child_map: int32 [128, 256], replicated, may hold values from -1 to 4095, as said below
- parent_list: int32 [128, 1], replicated, may hold values from 0 to 3; in each aligned block of 4 rows (0 to 3, 4 to 7, ...) at most 2 rows name the same one
Outputs:
- front_out: float32 [4, 4096, 4096], P('front', 'tile')
The draws below stay inside these ranges and needn't reach their ends.
Inputs may be any that keep to these rules, and one draw needn't show every extreme that they name: `child_map`: row c gives the parent-front row of each of the 256 rows of child c: live entries come first and are distinct, -1 marks padding, every row has 128 to 256 live entries, and its first entry is 4095. `parent_list`: in each aligned block of 4 rows no front is named more than 2 times.
All inputs are finite; a program needn't handle non-finite values.
Results may differ from the reference program's by a relative error of at most 0.0003.
Values may be sent and summed in bfloat16 or wider, within the bound.
A program may use at most 128 MiB of HBM per device.

```python
import math
import jax
import jax.numpy as jnp
import numpy as np
from jax import lax

FRONT = 4096
PANEL = 512
PANELS = 2
CHILD = 256
BLOCK_ROWS = 64
BLK_DEV = 4
CAPACITY = 2
NCHILD = 128
N_FRONT = 4


coupling_rank = 8


def draw_front_entries(key, part):
    key_noise = jax.random.fold_in(key, 0)
    key_diag = jax.random.fold_in(key, 1)
    key_coupling = jax.random.fold_in(key, 3)
    super_cols = PANELS * PANEL
    base_diag = 2.0 * FRONT ** 0.5
    uniform_part = jax.random.uniform(key_noise, (N_FRONT, FRONT, FRONT), jnp.float32, -1.0, 1.0)
    symmetric = 0.5 * (uniform_part + jnp.swapaxes(uniform_part, 1, 2))
    positions = jnp.arange(FRONT)
    amplitude = jnp.where(positions < super_cols, 1.0, 0.5).astype(jnp.float32) * (6.0 * base_diag / PANEL) ** 0.5
    coupling = jax.random.uniform(key_coupling, (N_FRONT, FRONT, coupling_rank), jnp.float32, -1.0, 1.0) * amplitude[None, :, None]
    low_rank = jnp.zeros((N_FRONT, FRONT, FRONT), jnp.float32)
    for mode_index in range(coupling_rank):
        column = coupling[:, :, mode_index]
        low_rank = low_rank + column[:, :, None] * column[:, None, :]
    diagonal = jax.random.uniform(key_diag, (N_FRONT, FRONT), jnp.float32, base_diag, 2.0 * base_diag)
    on_diag = positions[:, None] == positions[None, :]
    return jnp.where(on_diag[None], diagonal[:, :, None], symmetric) + low_rank


def draw_child_blocks(key, part):
    key_noise, key_diag = jax.random.split(key, 2)
    uniform_part = jax.random.uniform(key_noise, (NCHILD, CHILD, CHILD), jnp.float32, -0.5, 0.5)
    symmetric = 0.5 * (uniform_part + jnp.swapaxes(uniform_part, 1, 2))
    diagonal = jax.random.uniform(key_diag, (NCHILD, CHILD), jnp.float32, 1.5 * CHILD ** 0.5, 3.0 * CHILD ** 0.5)
    on_diag = jnp.arange(CHILD)[:, None] == jnp.arange(CHILD)[None, :]
    complete = jnp.where(on_diag[None], diagonal[:, :, None], symmetric)
    blocks = complete.reshape(NCHILD, CHILD // BLOCK_ROWS, BLOCK_ROWS, CHILD)
    return jnp.swapaxes(blocks, 0, 1).reshape(NCHILD * (CHILD // BLOCK_ROWS), BLOCK_ROWS, CHILD).astype(jnp.bfloat16)


def draw_child_map(key, part):
    child_keys = jax.random.split(key, NCHILD + 1)

    def one_child(child_key):
        shuffled = jax.random.permutation(child_key, FRONT - 1).astype(jnp.int32)
        return jnp.concatenate([jnp.full((1,), FRONT - 1, jnp.int32), shuffled[:CHILD - 1]])
    row_maps = jax.vmap(one_child)(child_keys[:NCHILD])
    live_count = jax.random.randint(child_keys[NCHILD], (NCHILD,), CHILD // 2, CHILD + 1).astype(jnp.int32)
    live_count = live_count.at[0].set(CHILD).at[1].set(CHILD // 2)
    position = jnp.arange(CHILD)[None, :]
    return jnp.where(position < live_count[:, None], row_maps, -1).astype(jnp.int32)


def shared_out(rng, own, number, rows, number_of, top, reach, lean):
    ranking = jax.random.permutation(rng, number_of)
    heavy_load, ordinary = shares(number_of, rows * top, reach, lean, True), shares(number_of, rows * top, reach, lean, False)
    places = jnp.arange(number_of)

    def named(tallies, turn):
        used = int((tallies > 0).sum())
        fixed = max(1, used // 4)
        moved = fixed + (places - fixed + turn * (used - fixed)) % max(1, number_of - fixed)
        return jnp.zeros((number_of,), jnp.int32).at[ranking[jnp.where(places < fixed, places, moved)]].set(jnp.asarray(tallies, jnp.int32))

    tallies = jnp.where(number % 4 == 0, named(heavy_load, number // 4), named(ordinary, number - number // 4 - 1))
    mixed = jax.random.permutation(jax.random.fold_in(own, 3), number_of)
    giver, taker = mixed[0:number_of // 2 * 2:2], mixed[1:number_of // 2 * 2:2]
    margin = jnp.minimum(tallies[giver] - 1, reach - tallies[taker]) // 2
    margin = jnp.where((giver == ranking[0]) | (taker == ranking[0]) | (tallies[taker] == 0), 0, jnp.maximum(margin, 0))
    moved = jax.random.randint(jax.random.fold_in(own, 4), (number_of // 2,), 0, 1 << 20) % (margin + 1)
    tallies = tallies.at[giver].add(-moved).at[taker].add(moved)
    members = jnp.searchsorted(jnp.cumsum(tallies), jnp.arange(rows * top), side="right").astype(jnp.int32)
    listing = members.reshape(top, rows).T
    listing = listing[jax.random.permutation(jax.random.fold_in(own, 1), rows)]
    turn = jax.random.randint(jax.random.fold_in(own, 2), (rows, 1), 0, top)
    return jnp.take_along_axis(listing, (jnp.arange(top)[None, :] + turn) % top, axis=1)


def shares(amount, total, reach, slope, full):
    loads = [(1 << 20) // math.isqrt(grade ** slope) + 1 for grade in range(1, amount + 1)]
    largest = reach if full else min(reach, max(-(-total // amount), total * loads[0] // sum(loads)))
    least = 1 if total - largest >= amount - 1 else 0
    given, spare = [largest] + [least] * (amount - 1), total - largest - least * (amount - 1)
    while spare > 0:
        free = [i for i in range(1, amount) if given[i] < largest] or [i for i in range(1, amount) if given[i] < reach]
        whole, left = sum([loads[i] for i in free]), spare
        for i in free:
            addition = min(reach - given[i], max(1, left * loads[i] // whole), spare)
            given[i] = given[i] + addition
            spare = spare - addition
    return np.array(given)


def setup_inputs(seed: int = 0) -> dict:
    key_list = jax.random.split(jax.random.key(seed), 5)
    front_entries = draw_front_entries(jax.random.fold_in(key_list[4], 71), 0)
    child_blocks = draw_child_blocks(jax.random.fold_in(key_list[4], 71), 0)
    child_map = draw_child_map(jax.random.fold_in(key_list[4], 71), 0)
    parent_list_keys = jax.random.split(jax.random.fold_in(key_list[3], 1), NCHILD // BLK_DEV)
    parent_list_turns = jax.random.permutation(jax.random.fold_in(key_list[3], 3), NCHILD // BLK_DEV)
    parent_list = jax.vmap(lambda own, number: shared_out(jax.random.fold_in(key_list[3], 2), own, number, BLK_DEV, N_FRONT, 1, CAPACITY, 2))(parent_list_keys, parent_list_turns).reshape((NCHILD, 1))
    return {"front_entries": front_entries, "child_blocks": child_blocks, "child_map": child_map, "parent_list": parent_list}


def factor_front(matrix):
    row_ids = jnp.arange(FRONT)[:, None]
    for panel_no in range(PANELS):
        left_col = panel_no * PANEL
        right_col = left_col + PANEL
        diag_factor = jnp.linalg.cholesky(matrix[left_col:right_col, left_col:right_col])
        lower_part = jax.scipy.linalg.solve_triangular(diag_factor, matrix[right_col:, left_col:right_col].T, lower=True).T
        remainder = matrix[right_col:, right_col:] - jnp.dot(lower_part, lower_part.T, precision=lax.Precision.HIGHEST)
        stacked = jnp.concatenate([jnp.zeros((left_col, PANEL), jnp.float32), diag_factor, lower_part], 0)
        in_lower = row_ids - left_col >= jnp.arange(PANEL)[None, :]
        panel_out = jnp.where(in_lower, stacked, matrix[:, left_col:right_col])
        matrix = matrix.at[:, left_col:right_col].set(panel_out)
        matrix = matrix.at[right_col:, right_col:].set(remainder)
    return matrix

def reference(front_entries, child_blocks, child_map, parent_list):
    row_blocks = CHILD // BLOCK_ROWS
    children = jnp.transpose(child_blocks.reshape(row_blocks, NCHILD, BLOCK_ROWS, CHILD), (1, 0, 2, 3)).reshape(NCHILD, CHILD, CHILD)
    places = jnp.where(child_map >= 0, child_map, FRONT).astype(jnp.int32)
    target = parent_list[:, 0].astype(jnp.int32)

    def add_child(child_id, extend_sum):
        spot_ids = places[child_id]
        return extend_sum.at[target[child_id], spot_ids[:, None], spot_ids[None, :]].add(children[child_id].astype(jnp.float32), mode='drop')
    extend_sum = lax.fori_loop(0, NCHILD, add_child, jnp.zeros((N_FRONT, FRONT, FRONT), jnp.float32))
    assembled = front_entries + extend_sum
    return lax.map(factor_front, assembled)
```

```python
import jax
import jax.numpy as jnp
from jax import lax
from jax.sharding import PartitionSpec as P

FRONT = 4096
PANEL = 512
PANELS = 2
CHILD = 256
BLOCK_ROWS = 64
BLK_DEV = 4
CAPACITY = 2


def routing(child_map, parent_list, front_count, tile_count, group_id):
    child_count = child_map.shape[0]
    fronts = jnp.arange(front_count, dtype=jnp.int32)
    target = parent_list[:, 0]
    blocks = (
        jnp.arange(front_count * tile_count, dtype=jnp.int32)[:, None] * BLK_DEV
        + jnp.arange(BLK_DEV, dtype=jnp.int32)[None, :]
    )
    child_of = blocks % child_count
    part_of = blocks // child_count
    child_ids = jnp.arange(child_count, dtype=jnp.int32)
    dest_front = jnp.sum(jnp.where(child_of[..., None] == child_ids, target, 0), axis=2)
    earlier = jnp.arange(BLK_DEV)[:, None] > jnp.arange(BLK_DEV)[None, :]
    same_dest = dest_front[:, :, None] == dest_front[:, None, :]
    slot_rank = jnp.sum(same_dest & earlier[None], axis=2)
    slot_ids = jnp.arange(CAPACITY, dtype=jnp.int32)
    select = (dest_front[:, None, None, :] == fronts[None, :, None, None]) & (
        slot_rank[:, None, None, :] == slot_ids[None, None, :, None]
    )
    to_group = select[:, group_id]
    slot_live = jnp.any(to_group, axis=2)
    slot_child = jnp.sum(jnp.where(to_group, child_of[:, None, :], 0), axis=2)
    slot_part = jnp.sum(jnp.where(to_group, part_of[:, None, :], 0), axis=2)
    return (select, slot_live, slot_child, slot_part)


def body(front_entries, child_blocks, child_map, parent_list):
    tile_count = lax.axis_size("tile")
    front_count = lax.axis_size("front")
    group_id = lax.axis_index("front")
    tile_id = lax.axis_index("tile")
    rows_dev = front_entries.shape[1]
    first_row = tile_id * rows_dev
    child_count = child_map.shape[0]
    select, slot_live, slot_child, slot_part = routing(
        child_map, parent_list, front_count, tile_count, group_id
    )
    self_dev = group_id * tile_count + tile_id
    own_select = select[self_dev].astype(jnp.bfloat16)
    outgoing = jnp.einsum(
        "dsj,jrk->dsrk", own_select, child_blocks, preferred_element_type=jnp.float32
    ).astype(jnp.bfloat16)
    incoming = lax.all_to_all(outgoing, "front", split_axis=0, concat_axis=0, tiled=True)
    child_hot = (slot_child[..., None] == jnp.arange(child_count, dtype=jnp.int32)).astype(
        jnp.float32
    )
    map_values = jnp.einsum(
        "dsn,nk->dsk", child_hot, child_map.astype(jnp.float32), precision=lax.Precision.HIGHEST
    )
    col_flat = map_values.astype(jnp.int32)
    part_count = CHILD // BLOCK_ROWS
    col_parts = col_flat.reshape(col_flat.shape[0], CAPACITY, part_count, BLOCK_ROWS)
    part_hot = slot_part[..., None] == jnp.arange(part_count, dtype=jnp.int32)
    row_maps = jnp.sum(jnp.where(part_hot[..., None], col_parts, 0), axis=2)
    row_valid = slot_live[..., None] & (row_maps >= 0)
    row_table = jnp.where(row_valid, row_maps, FRONT).reshape(
        front_count, tile_count, CAPACITY, BLOCK_ROWS
    )
    col_table = col_flat.reshape(front_count, tile_count, CAPACITY, CHILD)
    own_columns = first_row + jnp.arange(rows_dev)
    shards = lax.all_gather(incoming[None], "tile", axis=0, tiled=True)

    def extend_range(f_lo, f_count):
        front_ids = f_lo + jnp.arange(f_count, dtype=jnp.int32)

        def one_tile(tile_step, running):
            child_rows = lax.dynamic_index_in_dim(shards, tile_step, 0, keepdims=False)
            col_maps = lax.dynamic_index_in_dim(col_table, tile_step, 1, keepdims=False)
            matches = (col_maps[..., None] == own_columns[None, None, None, :]).astype(
                jnp.bfloat16
            )
            values = jnp.einsum(
                "gsrk,gskc->gsrc", child_rows, matches, preferred_element_type=jnp.float32
            ).astype(jnp.bfloat16)
            targets = lax.dynamic_index_in_dim(row_table, tile_step, 1, keepdims=False)
            row_hot = (targets[..., None] == front_ids).astype(jnp.bfloat16)
            return running + jnp.einsum(
                "gsrf,gsrc->fc", row_hot, values, preferred_element_type=jnp.float32
            )

        empty = jnp.zeros((f_count, rows_dev), jnp.float32)
        return lax.fori_loop(0, shards.shape[0], one_tile, empty)

    hi = lax.Precision.HIGHEST
    split = PANELS * PANEL
    left_cols = front_entries[0][:, :split] + extend_range(0, split).T
    gathered = lax.all_gather(left_cols.astype(jnp.bfloat16), "tile", axis=0, tiled=True)
    right_cols = front_entries[0][:, split:] + extend_range(split, FRONT - split).T
    matrix = jnp.concatenate([left_cols, right_cols], 1)
    row_ids = first_row + jnp.arange(rows_dev)
    eye = jnp.eye(PANEL, dtype=jnp.float32)
    below = gathered[:, :PANEL].astype(jnp.float32)
    pieces = []
    for panel_no in range(PANELS):
        left_col = panel_no * PANEL
        right_col = left_col + PANEL
        diag_factor = jnp.linalg.cholesky(below[:PANEL])
        inv_factor = jax.scipy.linalg.solve_triangular(diag_factor, eye, lower=True)
        lower_rows = below[PANEL:]
        cols_piece = matrix[:, :PANEL]
        own_lower = jnp.dot(cols_piece, inv_factor.T, precision=hi)
        slice_start = jnp.clip(first_row - left_col, 0, PANEL - rows_dev)
        diag_rows = lax.dynamic_slice_in_dim(diag_factor, slice_start, rows_dev, 0)
        own_rows = jnp.where((row_ids < right_col)[:, None], diag_rows, own_lower)
        trailing = jnp.where((row_ids >= right_col)[:, None], own_lower, 0.0)
        weights = jnp.dot(trailing, inv_factor, precision=hi)
        remainder = matrix[:, PANEL:] - jnp.dot(weights, lower_rows.T, precision=hi)
        in_lower = row_ids[:, None] - left_col >= jnp.arange(PANEL)[None, :]
        pieces.append(jnp.where(in_lower, own_rows, cols_piece))
        matrix = remainder
        if panel_no + 1 < PANELS:
            next_left = right_col
            next_cols = gathered[next_left:, next_left:next_left + PANEL].astype(jnp.float32)
            top_lower = lower_rows[:PANEL]
            coupling = jnp.dot(
                inv_factor.T,
                jnp.dot(inv_factor, top_lower.T, precision=hi),
                precision=hi,
            )
            below = next_cols - jnp.dot(lower_rows, coupling, precision=hi)
    pieces.append(matrix)
    return jnp.concatenate(pieces, 1)[None]


def solution(mesh):
    return jax.shard_map(
        body,
        mesh=mesh,
        in_specs=(P("front", "tile", None), P(("front", "tile"), None, None), P(), P()),
        out_specs=P("front", "tile", None),
        check_vma=False,
    )
```
